32 devices in a mesh: mode: 2 (over y), col: 16 (over z, x, core).
Axes of the slice: x: 2, y: 2, z: 4, core: 2. Of those that a mesh axis runs over, the one named last changes fastest.
Arguments:
- tensor: float32 [512, 16, 4096], P('mode', 'col'), may hold values from -15 to 15
- start_basis: float32 [512, 128], replicated, may hold values from -6 to 6
Outputs:
- factor: float32 [512, 512], replicated
- basis: float32 [512, 128], replicated
- core: float32 [128, 16, 4096], P(None, 'col', 'mode')
The draws below stay inside these ranges and needn't reach their ends.
All inputs are finite; a program needn't handle non-finite values.
Results may differ from the reference program's by a relative error of at most 0.00018.
Values sent between devices are 32-bit elements; how exact they have to be, the bound alone decides.
A program may use at most 64 MiB of HBM per device.

```python
import math
import jax
import jax.numpy as jnp
from jax import lax

I1 = 512
RANK = 128
J_LEN = 4096
POWER = 2
I2_LEN = 16


def draw_tensor(key, part):
    scale_key = jax.random.fold_in(key, 11)
    value_key = jax.random.fold_in(key, 23)
    scales = jnp.exp(jax.random.uniform(scale_key, (I1, 1, 1), jnp.float32, 0.0, math.log(2.0)))
    values = jnp.clip(jax.random.normal(value_key, (I1, I2_LEN, J_LEN), jnp.float32), -6.0, 6.0)
    return (scales * values).astype(jnp.float32)


def centred(rng, dims, width, reach, held_as=jnp.bfloat16):
    drawn = jax.random.normal(rng, dims, jnp.float32) * width
    return jnp.minimum(jnp.maximum(drawn, -reach), reach).astype(held_as)


def setup_inputs(seed: int = 0) -> dict:
    arg_keys = jax.random.split(jax.random.key(seed), 3)
    return {
        "tensor": draw_tensor(jax.random.fold_in(arg_keys[2], 71), 0),
        "start_basis": centred(arg_keys[1], (I1, RANK), 1.0, 6.0, jnp.float32),
    }


def lower_chol(matrix):
    return jnp.linalg.cholesky(matrix)

def orthonormal(image):
    small = lower_chol(jnp.dot(image.T.astype(jnp.float32), image.astype(jnp.float32), precision=lax.Precision.HIGHEST, preferred_element_type=jnp.float32))
    return jax.scipy.linalg.solve_triangular(small, image.T, lower=True).T

def reference(tensor, start_basis):
    unfolded = tensor.reshape(I1, -1)
    columns = unfolded.shape[1]
    gram = jnp.dot(unfolded.astype(jnp.float32), unfolded.T.astype(jnp.float32), precision=lax.Precision.HIGHEST, preferred_element_type=jnp.float32)
    factor = lower_chol(gram / columns)
    basis = start_basis
    for step in range(POWER):
        inner = jnp.dot(factor.T.astype(jnp.float32), basis.astype(jnp.float32), precision=lax.Precision.HIGHEST, preferred_element_type=jnp.float32)
        image = jnp.dot(factor.astype(jnp.float32), inner.astype(jnp.float32), precision=lax.Precision.HIGHEST, preferred_element_type=jnp.float32)
        basis = orthonormal(image)
    core = jnp.dot(basis.T.astype(jnp.float32), unfolded.astype(jnp.float32), precision=lax.Precision.HIGHEST, preferred_element_type=jnp.float32)
    return (factor, basis, core.reshape(RANK, I2_LEN, J_LEN))
```

```python
import functools

import jax
import jax.numpy as jnp
from jax import lax
from jax.experimental import pallas as pl
from jax.experimental.pallas import tpu as pltpu
from jax.sharding import PartitionSpec as P

POWER = 2
BLOCK = 128
PANEL = 8


def halves(value):
    high = value.astype(jnp.bfloat16)
    low = (value - high.astype(jnp.float32)).astype(jnp.bfloat16)
    return high, low


def contract(left, right, dims):
    return lax.dot_general(left, right, (dims, ((), ())), preferred_element_type=jnp.float32)


def exact(left, right, dims):
    return lax.dot_general(
        left, right, (dims, ((), ())), precision=lax.Precision.HIGHEST,
        preferred_element_type=jnp.float32,
    )


NN = ((1,), (0,))
NT = ((1,), (1,))
TN = ((0,), (0,))


def split3(value):
    high = value.astype(jnp.bfloat16).astype(jnp.float32)
    rest = value - high
    middle = rest.astype(jnp.bfloat16).astype(jnp.float32)
    return high, middle, rest - middle


def eliminate_panel(aug, j):
    size, width = aug.shape
    first = PANEL * j
    rows = [aug[first + t : first + t + 1, :] for t in range(PANEL)]
    entry = {}
    for t in range(PANEL):
        for s in range(t, PANEL):
            value = rows[t][:, first + s : first + s + 1]
            entry[s, t] = jnp.broadcast_to(value, (1, size))
    pivots = []
    for t in range(PANEL):
        pivot = entry[t, t]
        pivots.append(pivot)
        inverse = 1.0 / pivot
        for s in range(t + 1, PANEL):
            ratio = entry[s, t] * inverse
            for u in range(s, PANEL):
                entry[u, s] = entry[u, s] - ratio * entry[u, t]
            rows[s] = rows[s] - jnp.concatenate([ratio] * (width // size), axis=1) * rows[t]
    done = []
    for t in range(PANEL):
        scale = lax.rsqrt(pivots[t])
        done.append(rows[t] * jnp.concatenate([scale] * (width // size), axis=1))
    panel = jnp.concatenate(done, axis=0)
    aug[first : first + PANEL, :] = panel
    below = first + PANEL
    if below < size:
        high, middle, low = split3(panel)
        left = jnp.concatenate([high, high, middle, high, low, middle], axis=0).astype(jnp.bfloat16)
        right = jnp.concatenate([high, middle, high, low, high, middle], axis=0).astype(jnp.bfloat16)
        aug[below:size, :] = aug[below:size, :] - contract(left[:, below:size], right, TN)


def eliminate(augs):
    for j in range(BLOCK // PANEL):
        for aug in augs:
            eliminate_panel(aug, j)


def load_augmented(aug, matrix):
    size = matrix.shape[0]
    row = lax.broadcasted_iota(jnp.int32, (size, size), 0)
    column = lax.broadcasted_iota(jnp.int32, (size, size), 1)
    aug[:, 0:size] = matrix
    aug[:, size : 2 * size] = jnp.where(row == column, 1.0, 0.0).astype(jnp.float32)


def linear_kernel(columns, gram_ref, start_ref, flat_ref, factor_ref, basis_ref, core_ref, gram, work, image, aug_f, aug_b):
    size, rank = start_ref.shape
    blocks = size // BLOCK
    row = lax.broadcasted_iota(jnp.int32, (BLOCK, BLOCK), 0)
    column = lax.broadcasted_iota(jnp.int32, (BLOCK, BLOCK), 1)
    scale = 1.0 / columns
    scaled = gram_ref[...] * scale
    gram[...] = scaled
    work[...] = scaled

    for step in range(max(blocks, POWER)):
        augs = []
        if step < blocks:
            at = step * BLOCK
            load_augmented(aug_f, work[at : at + BLOCK, at : at + BLOCK])
            augs.append(aug_f)
        if step < POWER:
            source = start_ref if step == 0 else basis_ref
            image[...] = exact(gram[...], source[...], NN)
            load_augmented(aug_b, exact(image[...], image[...], TN))
            augs.append(aug_b)
        eliminate(augs)
        if step < POWER:
            basis_ref[...] = exact(image[...], aug_b[:, rank : 2 * rank], NT)
        if step < blocks:
            upper = jnp.where(row <= column, aug_f[:, 0:BLOCK], 0.0)
            factor_ref[at : at + BLOCK, at : at + BLOCK] = upper.T
            if step > 0:
                factor_ref[0:at, at : at + BLOCK] = jnp.zeros((at, BLOCK), jnp.float32)
            below = at + BLOCK
            if below < size:
                inverse = aug_f[:, BLOCK : 2 * BLOCK]
                left = exact(work[below:size, at : at + BLOCK], inverse, NT)
                factor_ref[below:size, at : at + BLOCK] = left
                work[below:size, below:size] = work[below:size, below:size] - exact(left, left, NT)

    high, low = halves(basis_ref[...])
    width = 512
    for start in range(0, flat_ref.shape[1], width):
        flat_high, flat_low = halves(flat_ref[:, start : start + width])
        core_ref[:, start : start + width] = (
            contract(high, flat_high, TN) + contract(high, flat_low, TN) + contract(low, flat_high, TN)
        )


def linear(columns, gram, start_basis, flat):
    size, rank = start_basis.shape
    vmem = pl.BlockSpec(memory_space=pltpu.VMEM)
    return pl.pallas_call(
        functools.partial(linear_kernel, columns),
        out_shape=(
            jax.ShapeDtypeStruct((size, size), jnp.float32),
            jax.ShapeDtypeStruct((size, rank), jnp.float32),
            jax.ShapeDtypeStruct((rank, flat.shape[1]), jnp.float32),
        ),
        in_specs=[vmem] * 3,
        out_specs=(vmem,) * 3,
        scratch_shapes=[
            pltpu.VMEM((size, size), jnp.float32),
            pltpu.VMEM((size, size), jnp.float32),
            pltpu.VMEM((size, rank), jnp.float32),
            pltpu.VMEM((BLOCK, 2 * BLOCK), jnp.float32),
            pltpu.VMEM((rank, 2 * rank), jnp.float32),
        ],
        name="linear",
    )(gram, start_basis, flat)


def matmul(left, right):
    return jnp.dot(left, right, precision=lax.Precision.HIGHEST, preferred_element_type=jnp.float32)


def per_device(tensor, start_basis):
    regrouped = lax.all_to_all(tensor, "mode", split_axis=2, concat_axis=0, tiled=True)
    rows = regrouped.shape[0]
    flat = regrouped.reshape(rows, -1)
    columns = flat.shape[1] * lax.axis_size("mode") * lax.axis_size("col")
    gram = matmul(flat, flat.T)
    total = lax.psum(gram, ("mode", "col"))
    factor, basis, core = linear(columns, total, start_basis, flat)
    return (factor, basis, core.reshape(basis.shape[1], regrouped.shape[1], regrouped.shape[2]))


def solution(mesh):
    in_specs = (P("mode", "col", None), P())
    out_specs = (P(), P(), P(None, "col", "mode"))
    return jax.shard_map(
        per_device, mesh=mesh, in_specs=in_specs, out_specs=out_specs, check_vma=False
    )
```

```python
import functools

import jax
import jax.numpy as jnp
from jax import lax
from jax.experimental import pallas as pl
from jax.experimental.pallas import tpu as pltpu
from jax.sharding import PartitionSpec as P

POWER = 2
BLOCK = 128
PANEL = 8
CHUNK = 512
MESH = pl.DeviceIdType.MESH


def halves(value):
    high = value.astype(jnp.bfloat16)
    low = (value - high.astype(jnp.float32)).astype(jnp.bfloat16)
    return high, low


def contract(left, right, dims):
    return lax.dot_general(left, right, (dims, ((), ())), preferred_element_type=jnp.float32)


def exact(left, right, dims):
    return lax.dot_general(
        left, right, (dims, ((), ())), precision=lax.Precision.HIGHEST,
        preferred_element_type=jnp.float32,
    )


NN = ((1,), (0,))
NT = ((1,), (1,))
TN = ((0,), (0,))


def split3(value):
    high = value.astype(jnp.bfloat16).astype(jnp.float32)
    rest = value - high
    middle = rest.astype(jnp.bfloat16).astype(jnp.float32)
    return high, middle, rest - middle


def eliminate_panel(aug, j):
    size, width = aug.shape
    first = PANEL * j
    rows = [aug[first + t : first + t + 1, :] for t in range(PANEL)]
    entry = {}
    for t in range(PANEL):
        for s in range(t, PANEL):
            value = rows[t][:, first + s : first + s + 1]
            entry[s, t] = jnp.broadcast_to(value, (1, size))
    pivots = []
    for t in range(PANEL):
        pivot = entry[t, t]
        pivots.append(pivot)
        inverse = 1.0 / pivot
        for s in range(t + 1, PANEL):
            ratio = entry[s, t] * inverse
            for u in range(s, PANEL):
                entry[u, s] = entry[u, s] - ratio * entry[u, t]
            rows[s] = rows[s] - jnp.concatenate([ratio] * (width // size), axis=1) * rows[t]
    done = []
    for t in range(PANEL):
        scale = lax.rsqrt(pivots[t])
        done.append(rows[t] * jnp.concatenate([scale] * (width // size), axis=1))
    panel = jnp.concatenate(done, axis=0)
    aug[first : first + PANEL, :] = panel
    below = first + PANEL
    if below < size:
        high, middle, low = split3(panel)
        left = jnp.concatenate([high, high, middle, high, low, middle], axis=0).astype(jnp.bfloat16)
        right = jnp.concatenate([high, middle, high, low, high, middle], axis=0).astype(jnp.bfloat16)
        aug[below:size, :] = aug[below:size, :] - contract(left[:, below:size], right, TN)


def eliminate(augs):
    for j in range(BLOCK // PANEL):
        for aug in augs:
            eliminate_panel(aug, j)


def load_augmented(aug, matrix):
    size = matrix.shape[0]
    row = lax.broadcasted_iota(jnp.int32, (size, size), 0)
    column = lax.broadcasted_iota(jnp.int32, (size, size), 1)
    aug[:, 0:size] = matrix
    aug[:, size : 2 * size] = jnp.where(row == column, 1.0, 0.0).astype(jnp.float32)


def lower_blocks(blocks):
    return [(i, k) for i in range(blocks) for k in range(i + 1)]


def stages_of(modes, cols):
    stages, stride = [], 1
    first = 2 if cols % 2 == 0 else 1
    if first > 1:
        stages.append((1, first, False))
        stride = first
    second = 2 if (cols // stride) % 2 == 0 else 1
    stages.append((stride, second, True))
    stride *= second
    if cols // stride > 1:
        stages.append((stride, cols // stride, False))
    return stages


def gather_kernel(modes, cols, x_ref, flat_ref, total_ref, acc, main, cross, *rest):
    mode, col = lax.axis_index("mode"), lax.axis_index("col")
    stages = stages_of(modes, cols)
    slots = rest[: len(stages)]
    own_sem, piece_send, piece_recv, sum_send, sum_recv, share_send, share_recv = rest[len(stages) :]
    rows, depth, length = x_ref.shape
    size = rows * modes
    width = length // modes
    chunk = min(CHUNK, width)
    per = width // chunk
    chunks = depth * per

    def position(stage):
        stride, count, with_mode = stage
        place = lax.rem(lax.div(col, stride), count)
        return place * modes + mode if with_mode else place

    def members(stage):
        return stage[1] * (modes if stage[2] else 1)

    def peer(stage, offset):
        stride, count, with_mode = stage
        other = lax.rem(position(stage) + offset, members(stage))
        place = lax.div(other, modes) if with_mode else other
        there = col + (place - lax.rem(lax.div(col, stride), count)) * stride
        return other, (lax.rem(other, modes) if with_mode else mode, there)

    partners = [(lax.rem(mode + d, modes), col) for d in range(1, modes)]
    greeted = [] if any(stage[2] for stage in stages) else list(partners)
    for stage in stages:
        greeted += [peer(stage, d)[1] for d in range(1, members(stage))]
    barrier = pltpu.get_barrier_semaphore()
    for device in greeted:
        pl.semaphore_signal(barrier, inc=1, device_id=device, device_id_type=MESH)
    pl.semaphore_wait(barrier, len(greeted))

    def spans(c):
        layer, part = lax.div(c, per), lax.rem(c, per)
        return layer, part * chunk, pl.multiple_of(layer * width + part * chunk, chunk)

    def piece(c, d):
        layer, start, target = spans(c)
        source = pl.multiple_of(lax.rem(mode + d, modes) * width + start, chunk)
        place = pl.ds(pl.multiple_of(mode * rows, rows), rows)
        return pltpu.make_async_remote_copy(
            src_ref=x_ref.at[:, layer, pl.ds(source, chunk)],
            dst_ref=flat_ref.at[place, pl.ds(target, chunk)],
            send_sem=piece_send.at[d - 1, c],
            recv_sem=piece_recv.at[d - 1, c],
            device_id=partners[d - 1],
            device_id_type=MESH,
        )

    def own(c):
        layer, start, target = spans(c)
        source = pl.multiple_of(mode * width + start, chunk)
        place = pl.ds(pl.multiple_of(mode * rows, rows), rows)
        return pltpu.make_async_copy(
            x_ref.at[:, layer, pl.ds(source, chunk)], flat_ref.at[place, pl.ds(target, chunk)], own_sem.at[c]
        )

    def begin(c, carry):
        for d in range(1, modes):
            piece(c, d).start()
        own(c).start()
        return carry

    lax.fori_loop(0, chunks, begin, 0)
    main[...] = jnp.zeros_like(main)
    cross[...] = jnp.zeros_like(cross)

    def accumulate(c, carry):
        own(c).wait()
        for d in range(1, modes):
            piece(c, d).wait_recv()
        target = spans(c)[2]
        high, low = halves(flat_ref[:, pl.ds(target, chunk)])
        main[...] += contract(high, high, NT)
        cross[...] += contract(high, low, NT)
        return carry

    lax.fori_loop(0, chunks, accumulate, 0)

    blocks = size // BLOCK
    pairs = lower_blocks(blocks)
    for n, (i, k) in enumerate(pairs):
        tall, wide = slice(i * BLOCK, (i + 1) * BLOCK), slice(k * BLOCK, (k + 1) * BLOCK)
        acc[n * BLOCK : (n + 1) * BLOCK, :] = main[tall, wide] + (cross[tall, wide] + cross[wide, tall].T)
    used = len(pairs) * BLOCK
    if used < acc.shape[0]:
        acc[used:, :] = jnp.zeros((acc.shape[0] - used, BLOCK), jnp.float32)

    base, extent = 0, acc.shape[0]
    bases = []
    for g, stage in enumerate(stages):
        count = members(stage)
        part = extent // count
        copies = []
        for d in range(1, count):
            other, device = peer(stage, d)
            copy = pltpu.make_async_remote_copy(
                src_ref=acc.at[pl.ds(pl.multiple_of(base + other * part, 8), part), :],
                dst_ref=slots[g].at[d - 1],
                send_sem=sum_send.at[g, d - 1],
                recv_sem=sum_recv.at[g, d - 1],
                device_id=device,
                device_id_type=MESH,
            )
            copy.start()
            copies.append(copy)
        base = base + position(stage) * part
        extent = part
        bases.append((base, part))
        for copy in copies:
            copy.wait()
        mine = pl.ds(pl.multiple_of(base, 8), part)
        added = acc[mine, :]
        for d in range(1, count):
            added = added + slots[g][d - 1]
        if g < len(stages) - 1:
            acc[mine, :] = added
        else:
            total_ref[mine, :] = added

    for g in reversed(range(len(stages))):
        stage = stages[g]
        base, part = bases[g]
        mine = pl.ds(pl.multiple_of(base, 8), part)
        copies = []
        for d in range(1, members(stage)):
            copy = pltpu.make_async_remote_copy(
                src_ref=total_ref.at[mine, :],
                dst_ref=total_ref.at[mine, :],
                send_sem=share_send.at[g, d - 1],
                recv_sem=share_recv.at[g, d - 1],
                device_id=peer(stage, d)[1],
                device_id_type=MESH,
            )
            copy.start()
            copies.append(copy)
        for copy in copies:
            copy.wait()

    def end(c, carry):
        for d in range(1, modes):
            piece(c, d).wait_send()
        return carry

    lax.fori_loop(0, chunks, end, 0)


def gather(tensor):
    modes, cols = lax.axis_size("mode"), lax.axis_size("col")
    rows, depth, length = tensor.shape
    size = rows * modes
    width = length // modes
    chunks = depth * (width // min(CHUNK, width))
    stages = stages_of(modes, cols)
    unit = 8 * modes * cols
    packed = -(-(len(lower_blocks(size // BLOCK)) * BLOCK) // unit) * unit
    slots, extent, most = [], packed, 1
    for stride, count, with_mode in stages:
        count = count * (modes if with_mode else 1)
        extent = extent // count
        most = max(most, count - 1)
        slots.append(pltpu.VMEM((max(count - 1, 1), extent, BLOCK), jnp.float32))
    dma = pltpu.SemaphoreType.DMA
    vmem = pl.BlockSpec(memory_space=pltpu.VMEM)
    return pl.pallas_call(
        functools.partial(gather_kernel, modes, cols),
        out_shape=(
            jax.ShapeDtypeStruct((size, depth * width), jnp.float32),
            jax.ShapeDtypeStruct((packed, BLOCK), jnp.float32),
        ),
        in_specs=[pl.BlockSpec(memory_space=pl.ANY)],
        out_specs=(vmem, vmem),
        scratch_shapes=[
            pltpu.VMEM((packed, BLOCK), jnp.float32),
            pltpu.VMEM((size, size), jnp.float32),
            pltpu.VMEM((size, size), jnp.float32),
            *slots,
            dma((chunks,)),
            dma((max(modes - 1, 1), chunks)),
            dma((max(modes - 1, 1), chunks)),
            *[dma((len(stages), most))] * 4,
        ],
        compiler_params=pltpu.CompilerParams(collective_id=0, has_side_effects=True),
        name="gather",
    )(tensor)


def linear_kernel(columns, packed_ref, start_ref, flat_ref, factor_ref, basis_ref, core_ref, gram, work, image, aug_f, aug_b):
    size, rank = start_ref.shape
    blocks = size // BLOCK
    row = lax.broadcasted_iota(jnp.int32, (BLOCK, BLOCK), 0)
    column = lax.broadcasted_iota(jnp.int32, (BLOCK, BLOCK), 1)
    scale = 1.0 / columns
    for n, (i, k) in enumerate(lower_blocks(blocks)):
        scaled = packed_ref[n * BLOCK : (n + 1) * BLOCK, :] * scale
        gram[i * BLOCK : (i + 1) * BLOCK, k * BLOCK : (k + 1) * BLOCK] = scaled
        work[i * BLOCK : (i + 1) * BLOCK, k * BLOCK : (k + 1) * BLOCK] = scaled
        if i != k:
            gram[k * BLOCK : (k + 1) * BLOCK, i * BLOCK : (i + 1) * BLOCK] = scaled.T

    for step in range(max(blocks, POWER)):
        augs = []
        if step < blocks:
            at = step * BLOCK
            load_augmented(aug_f, work[at : at + BLOCK, at : at + BLOCK])
            augs.append(aug_f)
        if step < POWER:
            source = start_ref if step == 0 else basis_ref
            image[...] = exact(gram[...], source[...], NN)
            load_augmented(aug_b, exact(image[...], image[...], TN))
            augs.append(aug_b)
        eliminate(augs)
        if step < POWER:
            basis_ref[...] = exact(image[...], aug_b[:, rank : 2 * rank], NT)
        if step < blocks:
            upper = jnp.where(row <= column, aug_f[:, 0:BLOCK], 0.0)
            factor_ref[at : at + BLOCK, at : at + BLOCK] = upper.T
            if step > 0:
                factor_ref[0:at, at : at + BLOCK] = jnp.zeros((at, BLOCK), jnp.float32)
            below = at + BLOCK
            if below < size:
                inverse = aug_f[:, BLOCK : 2 * BLOCK]
                left = exact(work[below:size, at : at + BLOCK], inverse, NT)
                factor_ref[below:size, at : at + BLOCK] = left
                work[below:size, below:size] = work[below:size, below:size] - exact(left, left, NT)

    high, low = halves(basis_ref[...])
    width = 512
    for start in range(0, flat_ref.shape[1], width):
        flat_high, flat_low = halves(flat_ref[:, start : start + width])
        core_ref[:, start : start + width] = (
            contract(high, flat_high, TN) + contract(high, flat_low, TN) + contract(low, flat_high, TN)
        )


def linear(columns, packed, start_basis, flat):
    size, rank = start_basis.shape
    vmem = pl.BlockSpec(memory_space=pltpu.VMEM)
    return pl.pallas_call(
        functools.partial(linear_kernel, columns),
        out_shape=(
            jax.ShapeDtypeStruct((size, size), jnp.float32),
            jax.ShapeDtypeStruct((size, rank), jnp.float32),
            jax.ShapeDtypeStruct((rank, flat.shape[1]), jnp.float32),
        ),
        in_specs=[vmem] * 3,
        out_specs=(vmem,) * 3,
        scratch_shapes=[
            pltpu.VMEM((size, size), jnp.float32),
            pltpu.VMEM((size, size), jnp.float32),
            pltpu.VMEM((size, rank), jnp.float32),
            pltpu.VMEM((BLOCK, 2 * BLOCK), jnp.float32),
            pltpu.VMEM((rank, 2 * rank), jnp.float32),
        ],
        name="linear",
    )(packed, start_basis, flat)


def per_device(tensor, start_basis):
    depth = tensor.shape[1]
    flat, packed = gather(tensor)
    columns = flat.shape[1] * lax.axis_size("mode") * lax.axis_size("col")
    factor, basis, core = linear(columns, packed, start_basis, flat)
    return (factor, basis, core.reshape(basis.shape[1], depth, -1))


def solution(mesh):
    in_specs = (P("mode", "col", None), P())
    out_specs = (P(), P(), P(None, "col", "mode"))
    return jax.shard_map(
        per_device, mesh=mesh, in_specs=in_specs, out_specs=out_specs, check_vma=False
    )
```

```python
import functools

import jax
import jax.numpy as jnp
from jax import lax
from jax.experimental import pallas as pl
from jax.experimental.pallas import tpu as pltpu
from jax.sharding import PartitionSpec as P

POWER = 2
BLOCK = 128
PANEL = 8
CHUNK = 512
MESH = pl.DeviceIdType.MESH


def halves(value):
    high = value.astype(jnp.bfloat16)
    low = (value - high.astype(jnp.float32)).astype(jnp.bfloat16)
    return high, low


def contract(left, right, dims):
    return lax.dot_general(left, right, (dims, ((), ())), preferred_element_type=jnp.float32)


def exact(left, right, dims):
    return lax.dot_general(
        left, right, (dims, ((), ())), precision=lax.Precision.HIGHEST,
        preferred_element_type=jnp.float32,
    )


NN = ((1,), (0,))
NT = ((1,), (1,))
TN = ((0,), (0,))


def split3(value):
    high = value.astype(jnp.bfloat16).astype(jnp.float32)
    rest = value - high
    middle = rest.astype(jnp.bfloat16).astype(jnp.float32)
    return high, middle, rest - middle


def eliminate_panel(aug, j):
    size, width = aug.shape
    first = PANEL * j
    rows = [aug[first + t : first + t + 1, :] for t in range(PANEL)]
    entry = {}
    for t in range(PANEL):
        for s in range(t, PANEL):
            value = rows[t][:, first + s : first + s + 1]
            entry[s, t] = jnp.broadcast_to(value, (1, size))
    pivots = []
    for t in range(PANEL):
        pivot = entry[t, t]
        pivots.append(pivot)
        inverse = 1.0 / pivot
        for s in range(t + 1, PANEL):
            ratio = entry[s, t] * inverse
            for u in range(s, PANEL):
                entry[u, s] = entry[u, s] - ratio * entry[u, t]
            rows[s] = rows[s] - jnp.concatenate([ratio] * (width // size), axis=1) * rows[t]
    done = []
    for t in range(PANEL):
        scale = lax.rsqrt(pivots[t])
        done.append(rows[t] * jnp.concatenate([scale] * (width // size), axis=1))
    panel = jnp.concatenate(done, axis=0)
    aug[first : first + PANEL, :] = panel
    below = first + PANEL
    if below < size:
        high, middle, low = split3(panel)
        left = jnp.concatenate([high, high, middle, high, low, middle], axis=0).astype(jnp.bfloat16)
        right = jnp.concatenate([high, middle, high, low, high, middle], axis=0).astype(jnp.bfloat16)
        aug[below:size, :] = aug[below:size, :] - contract(left[:, below:size], right, TN)


def eliminate(augs):
    for j in range(BLOCK // PANEL):
        for aug in augs:
            eliminate_panel(aug, j)


def load_augmented(aug, matrix):
    size = matrix.shape[0]
    row = lax.broadcasted_iota(jnp.int32, (size, size), 0)
    column = lax.broadcasted_iota(jnp.int32, (size, size), 1)
    aug[:, 0:size] = matrix
    aug[:, size : 2 * size] = jnp.where(row == column, 1.0, 0.0).astype(jnp.float32)


def lower_blocks(blocks):
    return [(i, k) for i in range(blocks) for k in range(i + 1)]


def stages_of(modes, cols):
    stages, stride = [], 1
    first = 2 if cols % 2 == 0 else 1
    if first > 1:
        stages.append((1, first, False))
        stride = first
    second = 2 if (cols // stride) % 2 == 0 else 1
    stages.append((stride, second, True))
    stride *= second
    if cols // stride > 1:
        stages.append((stride, cols // stride, False))
    return stages


def round_up(value, unit):
    return -(-value // unit) * unit


def layout_of(size, modes, cols):
    pairs = lower_blocks(size // BLOCK)
    rows = size // modes
    inner = []
    if rows % BLOCK == 0 and modes > 1:
        inner = lower_blocks(rows // BLOCK)
    per = rows // BLOCK
    extent = round_up(len(inner) * BLOCK, 8 * cols)
    where = {}
    for m in range(modes):
        for n, (i, k) in enumerate(inner):
            where[m * per + i, m * per + k] = m * extent + n * BLOCK
    outer = [pair for pair in pairs if pair not in where]
    for n, pair in enumerate(outer):
        where[pair] = modes * extent + n * BLOCK
    return where, inner, extent, outer, round_up(len(outer) * BLOCK, 8 * modes * cols)


def members_of(stages, modes):
    return [count * (modes if with_mode else 1) for _, count, with_mode in stages]


def gather_kernel(modes, cols, x_ref, flat_ref, total_ref, local, acc_in, acc_out, main, cross, *rest):
    mode, col = lax.axis_index("mode"), lax.axis_index("col")
    all_stages = stages_of(modes, cols)
    col_stages = [(stride, count, False) for stride, count, _ in all_stages]
    n = len(all_stages)
    slots_in, slots_out = rest[:n], rest[n : 2 * n]
    local_sem, piece_send, piece_recv, swap_send, swap_recv, in_sems, out_sems, share_in, share_out = rest[2 * n :]
    rows, depth, length = x_ref.shape
    size = rows * modes
    width = length // modes
    chunk = min(CHUNK, width)
    per = width // chunk
    chunks = depth * per
    where, inner, in_extent, outer, out_extent = layout_of(size, modes, cols)

    def position(stage):
        stride, count, with_mode = stage
        place = lax.rem(lax.div(col, stride), count)
        return place * modes + mode if with_mode else place

    def members(stage):
        return stage[1] * (modes if stage[2] else 1)

    def peer(stage, offset):
        stride, count, with_mode = stage
        other = lax.rem(position(stage) + offset, members(stage))
        place = lax.div(other, modes) if with_mode else other
        there = col + (place - lax.rem(lax.div(col, stride), count)) * stride
        return other, (lax.rem(other, modes) if with_mode else mode, there)

    partners = [(lax.rem(mode + d, modes), col) for d in range(1, modes)]
    greeted = []
    for stage in all_stages:
        greeted += [peer(stage, d)[1] for d in range(1, members(stage))]
    barrier = pltpu.get_barrier_semaphore()
    for device in greeted:
        pl.semaphore_signal(barrier, inc=1, device_id=device, device_id_type=MESH)
    pl.semaphore_wait(barrier, len(greeted))

    own_rows = pl.ds(pl.multiple_of(mode * rows, rows), rows)

    def spans(c):
        layer, part = lax.div(c, per), lax.rem(c, per)
        return layer, part * chunk, pl.multiple_of(layer * width + part * chunk, chunk)

    def piece(c, d):
        layer, start, target = spans(c)
        source = pl.multiple_of(lax.rem(mode + d, modes) * width + start, chunk)
        return pltpu.make_async_remote_copy(
            src_ref=x_ref.at[:, layer, pl.ds(source, chunk)],
            dst_ref=flat_ref.at[own_rows, pl.ds(target, chunk)],
            send_sem=piece_send.at[d - 1, c],
            recv_sem=piece_recv.at[d - 1, c],
            device_id=partners[d - 1],
            device_id_type=MESH,
        )

    def load(c):
        layer, part = lax.div(c, per * modes), lax.rem(c, per * modes)
        source = pl.multiple_of(part * chunk, chunk)
        target = pl.multiple_of(layer * length + part * chunk, chunk)
        return pltpu.make_async_copy(
            x_ref.at[:, layer, pl.ds(source, chunk)], local.at[:, pl.ds(target, chunk)], local_sem.at[c]
        ), target

    def begin(c, carry):
        for d in range(1, modes):
            piece(c, d).start()
        return carry

    def begin_load(c, carry):
        load(c)[0].start()
        return carry

    early = max(chunks // 2, 1)
    lax.fori_loop(0, early, begin, 0)
    lax.fori_loop(0, chunks * modes, begin_load, 0)

    main[...] = jnp.zeros_like(main)
    cross[...] = jnp.zeros_like(cross)

    def accumulate_in(c, carry):
        copy, target = load(c)
        copy.wait()
        if inner:
            high, low = halves(local[:, pl.ds(target, chunk)])
            main[0:rows, 0:rows] += contract(high, high, NT)
            cross[0:rows, 0:rows] += contract(high, low, NT)
        return carry

    lax.fori_loop(0, chunks * modes, accumulate_in, 0)
    for layer in range(depth):
        source = pl.multiple_of(layer * length + mode * width, chunk)
        flat_ref[own_rows, layer * width : (layer + 1) * width] = local[:, pl.ds(source, width)]

    def pack(acc, pairs, extent):
        for at, (i, k) in enumerate(pairs):
            tall, wide = slice(i * BLOCK, (i + 1) * BLOCK), slice(k * BLOCK, (k + 1) * BLOCK)
            acc[at * BLOCK : (at + 1) * BLOCK, :] = main[tall, wide] + (cross[tall, wide] + cross[wide, tall].T)
        used = len(pairs) * BLOCK
        if used < extent:
            acc[used:, :] = jnp.zeros((extent - used, BLOCK), jnp.float32)

    def scatter_sum(stages, acc, extent, slots, sems, target):
        base, bases = 0, []
        for g, stage in enumerate(stages):
            count = members(stage)
            part = extent // count
            copies = []
            for d in range(1, count):
                other, device = peer(stage, d)
                copy = pltpu.make_async_remote_copy(
                    src_ref=acc.at[pl.ds(pl.multiple_of(base + other * part, 8), part), :],
                    dst_ref=slots[g].at[d - 1],
                    send_sem=sems.at[0, g, d - 1],
                    recv_sem=sems.at[1, g, d - 1],
                    device_id=device,
                    device_id_type=MESH,
                )
                copy.start()
                copies.append(copy)
            base = base + position(stage) * part
            extent = part
            bases.append((base, part))
            for copy in copies:
                copy.wait()
            mine = pl.ds(pl.multiple_of(base, 8), part)
            added = acc[mine, :]
            for d in range(1, count):
                added = added + slots[g][d - 1]
            if g < len(stages) - 1:
                acc[mine, :] = added
            else:
                total_ref[pl.ds(pl.multiple_of(target + base, 8), part), :] = added
        return bases

    def share(stages, bases, targets, sems):
        for g in reversed(range(len(stages))):
            stage = stages[g]
            base, part = bases[g]
            copies = []
            for d in range(1, members(stage)):
                for t, target in enumerate(targets):
                    mine = pl.ds(pl.multiple_of(target + base, 8), part)
                    copy = pltpu.make_async_remote_copy(
                        src_ref=total_ref.at[mine, :],
                        dst_ref=total_ref.at[mine, :],
                        send_sem=sems.at[0, g, (d - 1) * len(targets) + t],
                        recv_sem=sems.at[1, g, (d - 1) * len(targets) + t],
                        device_id=peer(stage, d)[1],
                        device_id_type=MESH,
                    )
                    copy.start()
                    copies.append(copy)
            for copy in copies:
                copy.wait()

    def accumulate_out(c, carry):
        for d in range(1, modes):
            piece(c, d).wait_recv()
        high, low = halves(flat_ref[:, pl.ds(spans(c)[2], chunk)])
        if inner:
            for m in range(1, modes):
                tall, wide = slice(m * rows, (m + 1) * rows), slice(0, m * rows)
                main[tall, wide] += contract(high[tall, :], high[wide, :], NT) + contract(low[tall, :], high[wide, :], NT)
                cross[tall, wide] += contract(high[tall, :], low[wide, :], NT)
        else:
            main[...] += contract(high, high, NT)
            cross[...] += contract(high, low, NT)
        return carry

    swaps = []
    if inner:
        pack(acc_in, inner, in_extent)
        main[...] = jnp.zeros_like(main)
        cross[...] = jnp.zeros_like(cross)
        bases = scatter_sum(col_stages, acc_in, in_extent, slots_in, in_sems, mode * in_extent)
        base, part = bases[-1]
        mine = pl.ds(pl.multiple_of(mode * in_extent + base, 8), part)
        for d in range(1, modes):
            swap = pltpu.make_async_remote_copy(
                src_ref=total_ref.at[mine, :],
                dst_ref=total_ref.at[mine, :],
                send_sem=swap_send.at[d - 1],
                recv_sem=swap_recv.at[d - 1],
                device_id=partners[d - 1],
                device_id_type=MESH,
            )
            swap.start()
            swaps.append(swap)
    lax.fori_loop(early, chunks, begin, 0)
    lax.fori_loop(0, early, accumulate_out, 0)
    if inner:
        for swap in swaps:
            swap.wait()
        share(col_stages, bases, [m * in_extent for m in range(modes)], share_in)
    lax.fori_loop(early, chunks, accumulate_out, 0)

    pack(acc_out, outer, out_extent)
    bases = scatter_sum(all_stages, acc_out, out_extent, slots_out, out_sems, modes * in_extent)
    share(all_stages, bases, [modes * in_extent], share_out)

    def end(c, carry):
        for d in range(1, modes):
            piece(c, d).wait_send()
        return carry

    lax.fori_loop(0, chunks, end, 0)


def gather(tensor):
    modes, cols = lax.axis_size("mode"), lax.axis_size("col")
    rows, depth, length = tensor.shape
    size = rows * modes
    width = length // modes
    chunks = depth * (width // min(CHUNK, width))
    stages = stages_of(modes, cols)
    _, inner, in_extent, _, out_extent = layout_of(size, modes, cols)
    in_extent = max(in_extent, 8 * cols)
    slots_in, slots_out, extent_in, extent, most = [], [], in_extent, out_extent, 1
    for stride, count, with_mode in stages:
        extent_in = extent_in // count
        slots_in.append(pltpu.VMEM((max(count - 1, 1), extent_in, BLOCK), jnp.float32))
        count = count * (modes if with_mode else 1)
        extent = extent // count
        slots_out.append(pltpu.VMEM((max(count - 1, 1), extent, BLOCK), jnp.float32))
        most = max(most, count - 1)
    dma = pltpu.SemaphoreType.DMA
    vmem = pl.BlockSpec(memory_space=pltpu.VMEM)
    packed = (modes * in_extent if inner else 0) + out_extent
    return pl.pallas_call(
        functools.partial(gather_kernel, modes, cols),
        out_shape=(
            jax.ShapeDtypeStruct((size, depth * width), jnp.float32),
            jax.ShapeDtypeStruct((packed, BLOCK), jnp.float32),
        ),
        in_specs=[pl.BlockSpec(memory_space=pl.ANY)],
        out_specs=(vmem, vmem),
        scratch_shapes=[
            pltpu.VMEM((rows, depth * length), jnp.float32),
            pltpu.VMEM((in_extent, BLOCK), jnp.float32),
            pltpu.VMEM((out_extent, BLOCK), jnp.float32),
            pltpu.VMEM((size, size), jnp.float32),
            pltpu.VMEM((size, size), jnp.float32),
            *slots_in,
            *slots_out,
            dma((chunks * modes,)),
            *[dma((max(modes - 1, 1), chunks))] * 2,
            *[dma((max(modes - 1, 1),))] * 2,
            *[dma((2, len(stages), most))] * 2,
            dma((2, len(stages), most * modes)),
            dma((2, len(stages), most)),
        ],
        compiler_params=pltpu.CompilerParams(collective_id=0, has_side_effects=True),
        name="gather",
    )(tensor)


def linear_kernel(columns, where, packed_ref, start_ref, flat_ref, factor_ref, basis_ref, core_ref, gram, work, image, aug_f, aug_b, core, core_sem):
    size, rank = start_ref.shape
    blocks = size // BLOCK
    row = lax.broadcasted_iota(jnp.int32, (BLOCK, BLOCK), 0)
    column = lax.broadcasted_iota(jnp.int32, (BLOCK, BLOCK), 1)
    scale = 1.0 / columns
    for (i, k), at in where.items():
        scaled = packed_ref[at : at + BLOCK, :] * scale
        gram[i * BLOCK : (i + 1) * BLOCK, k * BLOCK : (k + 1) * BLOCK] = scaled
        work[i * BLOCK : (i + 1) * BLOCK, k * BLOCK : (k + 1) * BLOCK] = scaled
        if i != k:
            gram[k * BLOCK : (k + 1) * BLOCK, i * BLOCK : (i + 1) * BLOCK] = scaled.T

    for step in range(max(blocks, POWER)):
        augs = []
        if step < blocks:
            at = step * BLOCK
            load_augmented(aug_f, work[at : at + BLOCK, at : at + BLOCK])
            augs.append(aug_f)
        if step < POWER:
            source = start_ref if step == 0 else basis_ref
            image[...] = exact(gram[...], source[...], NN)
            load_augmented(aug_b, exact(image[...], image[...], TN))
            augs.append(aug_b)
        eliminate(augs)
        if step < POWER:
            basis_ref[...] = exact(image[...], aug_b[:, rank : 2 * rank], NT)
        if step < blocks:
            upper = jnp.where(row <= column, aug_f[:, 0:BLOCK], 0.0)
            factor_ref[at : at + BLOCK, at : at + BLOCK] = upper.T
            if step > 0:
                factor_ref[0:at, at : at + BLOCK] = jnp.zeros((at, BLOCK), jnp.float32)
            below = at + BLOCK
            if below < size:
                inverse = aug_f[:, BLOCK : 2 * BLOCK]
                left = exact(work[below:size, at : at + BLOCK], inverse, NT)
                factor_ref[below:size, at : at + BLOCK] = left
                work[below:size, below:size] = work[below:size, below:size] - exact(left, left, NT)

    high, low = halves(basis_ref[...])
    depth, length = core_ref.shape[1:]
    width = min(CHUNK, length)
    copies = []
    for start in range(0, depth * length, width):
        part = slice(start, start + width)
        flat_high, flat_low = halves(flat_ref[:, part])
        core[:, part] = contract(high, flat_high, TN) + contract(high, flat_low, TN) + contract(low, flat_high, TN)
        layer, offset = divmod(start, length)
        copy = pltpu.make_async_copy(
            core.at[:, part], core_ref.at[:, layer, offset : offset + width], core_sem.at[len(copies)]
        )
        copy.start()
        copies.append(copy)
    for copy in copies:
        copy.wait()


def linear(columns, depth, packed, start_basis, flat):
    size, rank = start_basis.shape
    length = flat.shape[1] // depth
    where = layout_of(size, lax.axis_size("mode"), lax.axis_size("col"))[0]
    vmem = pl.BlockSpec(memory_space=pltpu.VMEM)
    return pl.pallas_call(
        functools.partial(linear_kernel, columns, where),
        out_shape=(
            jax.ShapeDtypeStruct((size, size), jnp.float32),
            jax.ShapeDtypeStruct((size, rank), jnp.float32),
            jax.ShapeDtypeStruct((rank, depth, length), jnp.float32),
        ),
        in_specs=[vmem] * 3,
        out_specs=(vmem, vmem, pl.BlockSpec(memory_space=pl.ANY)),
        scratch_shapes=[
            pltpu.VMEM((size, size), jnp.float32),
            pltpu.VMEM((size, size), jnp.float32),
            pltpu.VMEM((size, rank), jnp.float32),
            pltpu.VMEM((BLOCK, 2 * BLOCK), jnp.float32),
            pltpu.VMEM((rank, 2 * rank), jnp.float32),
            pltpu.VMEM((rank, flat.shape[1]), jnp.float32),
            pltpu.SemaphoreType.DMA((flat.shape[1] // min(CHUNK, length),)),
        ],
        name="linear",
    )(packed, start_basis, flat)


def per_device(tensor, start_basis):
    depth = tensor.shape[1]
    flat, packed = gather(tensor)
    columns = flat.shape[1] * lax.axis_size("mode") * lax.axis_size("col")
    factor, basis, core = linear(columns, depth, packed, start_basis, flat)
    return (factor, basis, core)


def solution(mesh):
    in_specs = (P("mode", "col", None), P())
    out_specs = (P(), P(), P(None, "col", "mode"))
    return jax.shard_map(
        per_device, mesh=mesh, in_specs=in_specs, out_specs=out_specs, check_vma=False
    )
```
